32 devices in a mesh: dp: 4 (over z), tensor: 8 (over y, x, core).
Axes of the slice: x: 2, y: 2, z: 4, core: 2. Of those that a mesh axis runs over, the one named last changes fastest.
Arguments:
- grad_out: bfloat16 [256, 9216], P(('dp', 'tensor')), may hold values from -6 to 6
- head_out: bfloat16 [256, 6144], P('dp', 'tensor'), may hold values from -0.375 to 0.375
- weight: bfloat16 [9216, 6144], P(None, 'tensor'), may hold values from -0.078125 to 0.078125
Outputs:
- head_grad: bfloat16 [256, 6144], P('dp', 'tensor')
- weight_grad: float32 [9216, 6144], P('dp', 'tensor')
The draws below stay inside these ranges and needn't reach their ends.
All inputs are finite; a program needn't handle non-finite values.
Results may differ from the reference program's by a relative error of at most 0.001.
Values may be sent and summed in bfloat16 or wider, within the bound.
No kernel may reach another device: no remote copies, remote signals or barrier semaphores. Data moves between devices by JAX's collectives and lax.ppermute only.
A program may use at most 128 MiB of HBM per device.

```python
import jax
import jax.numpy as jnp
from jax import lax

D = 9216
HD = 6144
GROUP = 64
BLOCKS = 4
TOKENS = 256


def with_spikes(drawn, rng, source, target, parts, factor):
    def block_of(position):
        return (jnp.arange(drawn.shape[position]) // (drawn.shape[position] // parts)).reshape((-1,) + (1,) * (drawn.ndim - 1 - position))

    first = jax.random.permutation(rng, parts)[block_of(target)]
    second = (block_of(target) + parts // 2) % parts
    return jnp.where((block_of(source) == first) | (block_of(source) == second), factor * drawn, drawn)


def levels(stream_key, extent, shards, least, high):
    def one(dim, shards_of):
        steps = jax.random.uniform(jax.random.fold_in(jax.random.fold_in(stream_key, 6), dim), (shards_of,), jnp.float32, least / len(shards), high / len(shards))
        return jnp.repeat(jnp.exp(steps), extent[dim] // shards_of).reshape((-1,) + (1,) * (len(extent) - dim - 1))

    loudness = one(*shards[0])
    for cut in shards[1:]:
        loudness = loudness * one(*cut)
    return loudness


def centred(own_key, dims, scale, bound, split=(), dtype=jnp.bfloat16):
    loudness = levels(own_key, dims, split, -0.22, 0.18) if split else 1.0
    drawn = jax.random.normal(own_key, dims, jnp.float32) * scale * loudness
    return jnp.minimum(jnp.maximum(drawn, -bound), bound).astype(dtype)


def bell_draw_with(stream_key, extent, width, bound, cuts, heavy, kind=jnp.bfloat16):
    values = width * jax.random.normal(stream_key, extent, jnp.float32)
    if cuts:
        values = values * levels(stream_key, extent, cuts, -0.22, 0.18)
    return jnp.clip(with_spikes(values, jax.random.fold_in(stream_key, 3), *heavy), -bound, bound).astype(kind)


def setup_inputs(seed: int = 0) -> dict:
    keys = jax.random.split(jax.random.key(seed), 4)
    return {
        "grad_out": bell_draw_with(keys[0], (TOKENS, D), 1.0, 6.0, ((0, 32),), (0, 1, 32, 2.75)),
        "head_out": centred(keys[1], (TOKENS, HD), TOKENS ** -0.5, 0.375, ((0, 4), (1, 8))),
        "weight": centred(keys[2], (D, HD), HD ** -0.5, 0.078125, ((1, 8),)),
    }


def reference(grad_out, head_out, weight):
    head_grad = jnp.dot(grad_out, weight, preferred_element_type=jnp.float32).astype(jnp.bfloat16)
    grad_blocks = grad_out.reshape(BLOCKS, GROUP, D)
    head_blocks = head_out.reshape(BLOCKS, GROUP, HD)

    def accumulate(running, operands):
        block_grad = lax.dot_general(operands[0], operands[1], (((0,), (0,)), ((), ())), preferred_element_type=jnp.float32)
        return running + block_grad, None

    weight_grad, _ = lax.scan(accumulate, jnp.zeros((D, HD), jnp.float32), (grad_blocks, head_blocks))
    return head_grad, weight_grad
```

```python
import jax
import jax.numpy as jnp
from jax import lax
from jax.sharding import PartitionSpec as P


def partner(index, step, size):
    if size & (size - 1) == 0:
        return index ^ step
    return (index + step) % size


def origin(index, step, size):
    if size & (size - 1) == 0:
        return jnp.bitwise_xor(index, step)
    return lax.rem(index - step + size, size)


def exchange(value, axis, step, size):
    pairs = [(i, partner(i, step, size)) for i in range(size)]
    return lax.ppermute(value, axis, pairs)


def body(grad_out, head_out, weight, sizes):
    blocks, lanes = sizes
    rows, width = grad_out.shape
    part = width // blocks
    dp = lax.axis_index("dp")
    lane = lax.axis_index("tensor")

    def columns(of):
        return lax.dynamic_slice_in_dim(grad_out, of * part, part, axis=1)

    def target(step):
        if blocks & (blocks - 1) == 0:
            return jnp.bitwise_xor(dp, step)
        return lax.rem(dp + step, blocks)

    def spread(value):
        across = [exchange(value, "tensor", 2 * k, lanes) if k else value for k in range(lanes // 2)]
        own = jnp.stack(across)
        other = lax.ppermute(own, "tensor", [(i, i ^ 1) for i in range(lanes)])
        return own, other

    far = jnp.concatenate([exchange(columns(target(k)), "dp", k, blocks) for k in range(1, blocks)], axis=0)
    near_own, near_other = spread(grad_out)
    heads = [head_out] + [exchange(head_out, "dp", k, blocks) for k in range(1, blocks)]
    far_own, far_other = spread(far)

    near = jnp.concatenate([near_own, near_other], axis=0)
    product = jnp.dot(near.reshape(lanes * rows, width), weight, preferred_element_type=jnp.float32)
    order = jnp.array([origin_of(lane, k, c, lanes) for c in range(2) for k in range(lanes // 2)])
    where = jnp.argsort(order)
    head_grad = product.astype(jnp.bfloat16).reshape(lanes, rows, -1)[where].reshape(lanes * rows, -1)

    mine = lax.dynamic_slice_in_dim(near, dp * part, part, axis=2)
    far_all = jnp.concatenate([far_own, far_other], axis=0)
    left = jnp.concatenate([mine, far_all], axis=1)
    right = jnp.stack(heads).reshape(blocks, lanes, rows, -1)[:, order]
    right = right.transpose(1, 0, 2, 3)
    weight_grad = lax.dot_general(
        left.reshape(-1, part), right.reshape(lanes * blocks * rows, -1), (((0,), (0,)), ((), ())), preferred_element_type=jnp.float32
    )
    return head_grad, weight_grad


def origin_of(lane, step, core, lanes):
    return jnp.bitwise_xor(origin(lane, 2 * step, lanes), core)


def solution(mesh):
    sizes = (mesh.shape["dp"], mesh.shape["tensor"])
    return jax.shard_map(
        lambda g, h, w: body(g, h, w, sizes),
        mesh=mesh,
        in_specs=(P(("dp", "tensor"), None), P("dp", "tensor"), P(None, "tensor")),
        out_specs=(P("dp", "tensor"), P("dp", "tensor")),
        check_vma=False,
    )
```
